32 devices in a mesh: space: 8 (over z, y), view: 4 (over x, core).
Axes of the slice: x: 2, y: 2, z: 4, core: 2. Of those that a mesh axis runs over, the one named last changes fastest.
Arguments:
- params: float32 [59, 16384], P(None, 'space'), may hold values from -8 to 514, as said below
- visible: int32 [8, 128, 16], P('space'), may hold values from 0 to 2047, as said below
- blocks: int32 [8, 128], P('space'), may hold values from 0 to 63, as said below
- counts: int32 [8, 8], P('space'), may hold values from 1 to 16
- depth_rank: int32 [4, 8], P('view'), may hold values from 0 to 7, each once within a row
- camera: float32 [4, 3], P('view'), may hold values from -0.006 to 0.006
- background: float32 [4, 3], P('view'), may hold values from 0 to 1
- target: float32 [4, 3, 128, 512], P('view', None, 'space'), may hold values from 0 to 1
Outputs:
- grad_params: float32 [59, 16384], P(None, 'space')
- rendered: float32 [4, 3, 128, 512], P('view', None, 'space')
- loss: float32 [4], P('view')
The draws below stay inside these ranges and needn't reach their ends.
Inputs may be any that keep to these rules, and one draw needn't show every extreme that they name: `visible`: each row of a subspace's table lists 16 different splats of that subspace in increasing order; every splat of the subspace is listed exactly once. Slot j of a subspace goes to owner j // 16; the 16 slots that one subspace sends to one owner name different blocks. counts[s, o] live slots lead the 16 slots that subspace s sends to owner o. `params`: rows 6 to 9 of a column hold a quaternion whose first component lies in [1, 2].
All inputs are finite; a program needn't handle non-finite values.
Results may differ from the reference program's by a relative error of at most 0.0003.
Values sent between devices are 32-bit elements; how exact they have to be, the bound alone decides.
A program may use at most 64 MiB of HBM per device.

```python
import math
import jax
import jax.numpy as jnp
from jax import lax

K = 16
SEG_DEV = 128
ROWS_DEV = 16
IMG_W = 512
SUBS = 8
VIEWS = 4
CAP = 16
SPL = 2048
HEIGHT = 128
BLK_DEV = 64
N_VIEW = 4


def layout(key):
    base_key = jax.random.fold_in(key, 7)
    key_blocks, key_lists = jax.random.split(base_key)
    scores = jax.random.randint(key_blocks, (SUBS, SUBS, BLK_DEV), 0, 1 << 20) * BLK_DEV + jnp.arange(BLK_DEV)[None, None, :]
    chosen = jnp.argsort(scores, axis=-1)[:, :, :CAP].astype(jnp.int32).reshape(SUBS, SEG_DEV)
    rank_keys = jax.random.randint(key_lists, (SUBS, SPL), 0, 1 << 16) * SPL + jnp.arange(SPL)[None, :]
    listing = jnp.argsort(rank_keys, axis=-1).astype(jnp.int32)
    return (chosen, listing)


def draw_visible(key, part):
    chosen, listing = layout(key)
    return jnp.sort(listing.reshape(SUBS, SEG_DEV, K), axis=-1).astype(jnp.int32)


def draw_blocks(key, part):
    chosen, listing = layout(key)
    return chosen


def draw_params(key, part):
    chosen, listing = layout(key)
    home_slot = jnp.argsort(listing, axis=-1).astype(jnp.int32) // K
    home_owner = home_slot // CAP
    home_block = jnp.take_along_axis(chosen, home_slot, axis=1)
    corner_y = (home_owner * ROWS_DEV + home_block // (IMG_W // 16) * 8).astype(jnp.float32)
    corner_x = (home_block % (IMG_W // 16) * 16).astype(jnp.float32)
    subkeys = jax.random.split(jax.random.fold_in(key, 3), 8)
    grid_shape = (SUBS, SPL)
    pos_x = corner_x + jax.random.uniform(subkeys[0], grid_shape, jnp.float32, -2.0, 18.0)
    pos_y = corner_y + jax.random.uniform(subkeys[1], grid_shape, jnp.float32, -2.0, 10.0)
    depths = jax.random.uniform(subkeys[2], grid_shape, jnp.float32, -8.0, 8.0)
    log_scale = jax.random.uniform(subkeys[3], (3, SUBS, SPL), jnp.float32, 0.0, 1.8)
    quat_real = jax.random.uniform(subkeys[4], grid_shape, jnp.float32, 1.0, 2.0)
    quat_rest = jax.random.uniform(subkeys[5], (3, SUBS, SPL), jnp.float32, -1.0, 1.0)
    logits = jax.random.uniform(subkeys[6], grid_shape, jnp.float32, -2.0, 3.0)
    harmonic = jnp.clip(0.3 * jax.random.normal(subkeys[7], (48, SUBS, SPL), jnp.float32), -1.2, 1.2)
    stacked = jnp.concatenate([pos_x[None], pos_y[None], depths[None], log_scale, quat_real[None], quat_rest, logits[None], harmonic], axis=0)
    return stacked.reshape(59, SUBS * SPL).astype(jnp.float32)


def with_ends(values, own_key, least, top_value):
    dims = values.shape
    index_at = [jax.random.randint(jax.random.fold_in(own_key, axis), (), 0, dims[axis]) for axis in range(len(dims))]
    values = values.at[tuple(index_at)].set(least)
    longest = dims.index(max(dims))
    index_at[longest] = (index_at[longest] + 1) % dims[longest]
    return values.at[tuple(index_at)].set(top_value)


def level_of(stream_key, dims, cuts, low, largest):
    gain = 1.0
    for axis_at, parts in cuts:
        steps = jax.random.uniform(jax.random.fold_in(jax.random.fold_in(stream_key, 6), axis_at), (parts,), jnp.float32, low / len(cuts), largest / len(cuts))
        gain = gain * jnp.repeat(jnp.exp(steps), dims[axis_at] // parts).reshape((-1,) + (1,) * (len(dims) - 1 - axis_at))
    return gain


def setup_inputs(seed: int = 0) -> dict:
    key_list = jax.random.split(jax.random.key(seed), 9)
    return {
        "params": draw_params(jax.random.fold_in(key_list[8], 71), 0),
        "visible": draw_visible(jax.random.fold_in(key_list[8], 71), 0),
        "blocks": draw_blocks(jax.random.fold_in(key_list[8], 71), 0),
        "counts": with_ends(jax.random.randint(key_list[3], (SUBS, SUBS), 1, CAP + 1), jax.random.fold_in(key_list[3], 1), 1, CAP).astype(jnp.int32),
        "depth_rank": jax.vmap(lambda own: jax.random.permutation(own, SUBS))(jax.random.split(key_list[4], VIEWS)).reshape((VIEWS, SUBS)).astype(jnp.int32),
        "camera": jnp.clip(jax.random.uniform(key_list[5], (VIEWS, 3), jnp.float32, -0.006, 0.006) * level_of(key_list[5], (VIEWS, 3), ((0, 4),), -0.4, 0.0), -0.006, 0.006),
        "background": jnp.clip(1.0 * jax.random.uniform(key_list[6], (VIEWS, 3), jnp.float32) ** level_of(key_list[6], (VIEWS, 3), ((0, 4),), -0.2, 0.2), 0.0, 1.0),
        "target": jnp.clip(1.0 * jax.random.uniform(key_list[7], (VIEWS, 3, HEIGHT, IMG_W), jnp.float32) ** level_of(key_list[7], (VIEWS, 3, HEIGHT, IMG_W), ((0, 4), (2, 8)), -0.2, 0.2), 0.0, 1.0),
    }


HIGHEST = lax.Precision.HIGHEST
SH_ZERO = 0.28209479177387814
SH_ONE = 0.4886025119029199
SH_TWO = (1.0925484305920792, -1.0925484305920792, 0.31539156525252005, -1.0925484305920792, 0.5462742152960396)
SH_THREE = (-0.5900435899266435, 2.890611442640554, -0.4570457994644658, 0.3731763325901154, -0.4570457994644658, 1.445305721320277, -0.5900435899266435)
DILATION = 0.3
SMOOTHING = 0.0001
SSIM_FIRST = 0.0001
SSIM_SECOND = 0.0009

def camera_rotation(angles):
    cos_a, sin_a = (jnp.cos(angles[0]), jnp.sin(angles[0]))
    cos_b, sin_b = (jnp.cos(angles[1]), jnp.sin(angles[1]))
    cos_c, sin_c = (jnp.cos(angles[2]), jnp.sin(angles[2]))
    unity = jnp.ones_like(cos_a)
    nought = jnp.zeros_like(cos_a)
    turn_x = jnp.stack([jnp.stack([unity, nought, nought]), jnp.stack([nought, cos_a, -sin_a]), jnp.stack([nought, sin_a, cos_a])])
    turn_y = jnp.stack([jnp.stack([cos_b, nought, sin_b]), jnp.stack([nought, unity, nought]), jnp.stack([-sin_b, nought, cos_b])])
    turn_z = jnp.stack([jnp.stack([cos_c, -sin_c, nought]), jnp.stack([sin_c, cos_c, nought]), jnp.stack([nought, nought, unity])])
    return jnp.dot(jnp.dot(turn_z, turn_y, precision=HIGHEST), turn_x, precision=HIGHEST)

def harmonics(view_axis):
    axis_x, axis_y, axis_z = (view_axis[0], view_axis[1], view_axis[2])
    sq_x, sq_y, sq_z = (axis_x * axis_x, axis_y * axis_y, axis_z * axis_z)
    values = [SH_ZERO * jnp.ones_like(axis_x), -SH_ONE * axis_y, SH_ONE * axis_z, -SH_ONE * axis_x, SH_TWO[0] * axis_x * axis_y, SH_TWO[1] * axis_y * axis_z, SH_TWO[2] * (2.0 * sq_z - sq_x - sq_y), SH_TWO[3] * axis_x * axis_z, SH_TWO[4] * (sq_x - sq_y), SH_THREE[0] * axis_y * (3.0 * sq_x - sq_y), SH_THREE[1] * axis_x * axis_y * axis_z, SH_THREE[2] * axis_y * (4.0 * sq_z - sq_x - sq_y), SH_THREE[3] * axis_z * (2.0 * sq_z - 3.0 * sq_x - 3.0 * sq_y), SH_THREE[4] * axis_x * (4.0 * sq_z - sq_x - sq_y), SH_THREE[5] * axis_z * (sq_x - sq_y), SH_THREE[6] * axis_x * (sq_x - 3.0 * sq_y)]
    return jnp.stack(values)

def project(param_in, angles, centre_x, centre_y):
    turn = camera_rotation(angles)
    scales = jnp.exp(param_in[3:6])
    quaternion = param_in[6:10]
    quaternion = quaternion / jnp.sqrt(lax.optimization_barrier(jnp.sum(quaternion * quaternion, axis=0)))
    part_w, part_x, part_y, part_z = (quaternion[0], quaternion[1], quaternion[2], quaternion[3])
    spin = [[1.0 - 2.0 * (part_y * part_y + part_z * part_z), 2.0 * (part_x * part_y - part_w * part_z), 2.0 * (part_x * part_z + part_w * part_y)], [2.0 * (part_x * part_y + part_w * part_z), 1.0 - 2.0 * (part_x * part_x + part_z * part_z), 2.0 * (part_y * part_z - part_w * part_x)], [2.0 * (part_x * part_z - part_w * part_y), 2.0 * (part_y * part_z + part_w * part_x), 1.0 - 2.0 * (part_x * part_x + part_y * part_y)]]
    frame = [[(turn[row, 0] * spin[0][col] + turn[row, 1] * spin[1][col] + turn[row, 2] * spin[2][col]) * scales[col] for col in range(3)] for row in range(2)]
    cov_xx = frame[0][0] * frame[0][0] + frame[0][1] * frame[0][1] + frame[0][2] * frame[0][2] + DILATION
    cov_xy = frame[0][0] * frame[1][0] + frame[0][1] * frame[1][1] + frame[0][2] * frame[1][2]
    cov_yy = frame[1][0] * frame[1][0] + frame[1][1] * frame[1][1] + frame[1][2] * frame[1][2] + DILATION
    determinant = cov_xx * cov_yy - cov_xy * cov_xy
    shift_x = param_in[0] - centre_x
    shift_y = param_in[1] - centre_y
    mean_u = turn[0, 0] * shift_x + turn[0, 1] * shift_y + turn[0, 2] * param_in[2] + centre_x
    mean_w = turn[1, 0] * shift_x + turn[1, 1] * shift_y + turn[1, 2] * param_in[2] + centre_y
    opacity = jax.nn.sigmoid(param_in[10])
    basis = harmonics(turn[2])
    coeffs = param_in[11:59].reshape(16, 3, param_in.shape[1])
    colour = 0.5 + lax.optimization_barrier(jnp.sum(basis[:, None, None] * coeffs, axis=0))
    record = jnp.stack([mean_u, mean_w, cov_yy / determinant, -cov_xy / determinant, cov_xx / determinant, opacity])
    return jnp.concatenate([record, colour], axis=0)

def render(gathered, grid_x, grid_y):
    delta_x = grid_x[:, None, :] - gathered[0][:, :, None]
    delta_y = grid_y[:, None, :] - gathered[1][:, :, None]
    powers = 0.5 * (gathered[2][:, :, None] * delta_x * delta_x + 2.0 * gathered[3][:, :, None] * delta_x * delta_y + gathered[4][:, :, None] * delta_y * delta_y)
    alphas = gathered[5][:, :, None] * jnp.exp(-powers)
    kept_log = jnp.log1p(-alphas)
    before = jnp.cumsum(kept_log, axis=1) - kept_log
    weights = alphas * jnp.exp(before)
    colour = jnp.einsum('skp,csk->scp', weights, gathered[6:9], precision=HIGHEST)
    return jnp.concatenate([colour, lax.optimization_barrier(jnp.sum(kept_log, axis=1))[:, None, :]], axis=1)

def pixel_grid(owners, blocks_used, strip_rows, block_cols):
    inner = jnp.arange(128).astype(jnp.int32)
    corner_y = owners * strip_rows + blocks_used // block_cols * 8
    corner_x = blocks_used % block_cols * 16
    grid_y = (corner_y[:, None] + inner[None, :] // 16).astype(jnp.float32) + 0.5
    grid_x = (corner_x[:, None] + inner[None, :] % 16).astype(jnp.float32) + 0.5
    return (grid_x, grid_y)

def composite(pieces, target_ids, depth_ranks, backdrop, block_rows, block_cols):
    block_count = block_rows * block_cols
    onehot = (target_ids[:, :, None] == jnp.arange(block_count).astype(jnp.int32)[None, None, :]).astype(jnp.float32)
    dense = jnp.einsum('scb,scqp->bsqp', onehot, pieces, precision=HIGHEST)
    kept_log = dense[:, :, 3]
    nearer = (depth_ranks[None, :] < depth_ranks[:, None]).astype(jnp.float32)
    before = jnp.einsum('st,btp->bsp', nearer, kept_log, precision=HIGHEST)
    picture = jnp.einsum('bsp,bscp->bcp', jnp.exp(before), dense[:, :, 0:3], precision=HIGHEST)
    picture = picture + backdrop[None, :, None] * jnp.exp(lax.optimization_barrier(jnp.sum(kept_log, axis=1)))[:, None, :]
    picture = picture.reshape(block_rows, block_cols, 3, 8, 16).transpose(2, 0, 3, 1, 4)
    return picture.reshape(3, block_rows * 8, block_cols * 16)

def blur_taps():
    raw_taps = [math.exp(-(offset - 5) * (offset - 5) / 4.5) for offset in range(11)]
    total = sum(raw_taps)
    return [value / total for value in raw_taps]

def blur(values, count):
    taps = blur_taps()
    width_px = values.shape[2]
    padded = jnp.pad(values, ((0, 0), (0, 0), (5, 5)))
    across = taps[0] * padded[:, :, 0:width_px]
    for offset in range(1, 11):
        across = across + taps[offset] * padded[:, :, offset:offset + width_px]
    result = taps[0] * across[:, 0:count]
    for offset in range(1, 11):
        result = result + taps[offset] * across[:, offset:offset + count]
    return result

def pixel_terms(picture, goal, count):
    mean_a = blur(picture, count)
    mean_b = blur(goal, count)
    var_a = blur(picture * picture, count) - mean_a * mean_a
    var_b = blur(goal * goal, count) - mean_b * mean_b
    cov_ab = blur(picture * goal, count) - mean_a * mean_b
    ssim = (2.0 * mean_a * mean_b + SSIM_FIRST) * (2.0 * cov_ab + SSIM_SECOND) / ((mean_a * mean_a + mean_b * mean_b + SSIM_FIRST) * (var_a + var_b + SSIM_SECOND))
    differ = picture[:, 5:5 + count] - goal[:, 5:5 + count]
    return 0.8 * jnp.sqrt(differ * differ + SMOOTHING) + 0.2 * (1.0 - ssim)

def reference(params, visible, blocks, counts, depth_rank, camera, background, target):
    subs_count = visible.shape[0]
    slot_total = visible.shape[1]
    capacity = slot_total // subs_count
    height_px = ROWS_DEV * subs_count
    width_px = IMG_W
    block_rows = ROWS_DEV // 8
    block_cols = IMG_W // 16
    slot_owner = (jnp.arange(slot_total) // capacity).astype(jnp.int32)
    live = jnp.arange(capacity).astype(jnp.int32)[None, None, :] < counts[:, :, None]
    target_ids = jnp.where(live, blocks.reshape(subs_count, subs_count, capacity), -1).astype(jnp.int32)
    grad_total = jnp.zeros(params.shape, jnp.float32)
    pictures = []
    losses = []
    for view_index in range(N_VIEW):

        def view_sum(param_in):
            records = project(param_in, camera[view_index], 0.5 * width_px, 0.5 * height_px)

            def one_sender(sender):
                local = lax.dynamic_slice_in_dim(records, sender * SPL, SPL, 1)
                lists = lax.dynamic_index_in_dim(visible, sender, 0, keepdims=False)
                slot_blocks = lax.dynamic_index_in_dim(blocks, sender, 0, keepdims=False)
                grid_x, grid_y = pixel_grid(slot_owner, slot_blocks, ROWS_DEV, block_cols)
                return render(local[:, lists], grid_x, grid_y)
            segments = lax.map(jax.checkpoint(one_sender), jnp.arange(subs_count).astype(jnp.int32))
            segments = segments.reshape(subs_count, subs_count, capacity, 4, 128)

            def one_owner(owner):
                pieces = lax.dynamic_index_in_dim(segments, owner, 1, keepdims=False)
                owned_ids = lax.dynamic_index_in_dim(target_ids, owner, 1, keepdims=False)
                return composite(pieces, owned_ids, depth_rank[view_index], background[view_index], block_rows, block_cols)
            strips = lax.map(jax.checkpoint(one_owner), jnp.arange(subs_count).astype(jnp.int32))
            picture = strips.transpose(1, 0, 2, 3).reshape(3, height_px, width_px)
            padded = jnp.pad(picture, ((0, 0), (5, 5), (0, 0)))
            goal = jnp.pad(target[view_index], ((0, 0), (5, 5), (0, 0)))
            return (jnp.sum(pixel_terms(padded, goal, height_px)), picture)
        (view_total, picture), view_grad = jax.value_and_grad(view_sum, has_aux=True)(params)
        grad_total = grad_total + view_grad
        pictures.append(picture)
        losses.append(view_total / (3.0 * height_px * width_px))
    return (grad_total, jnp.stack(pictures), jnp.stack(losses))
```

```python
import functools
import math

import jax
import jax.numpy as jnp
from jax import lax
from jax.experimental import pallas as pl
from jax.experimental.pallas import tpu as pltpu
from jax.sharding import PartitionSpec as P

HIGHEST = lax.Precision.HIGHEST
SH_ZERO = 0.28209479177387814
SH_ONE = 0.4886025119029199
SH_TWO = (
    1.0925484305920792,
    -1.0925484305920792,
    0.31539156525252005,
    -1.0925484305920792,
    0.5462742152960396,
)
SH_THREE = (
    -0.5900435899266435,
    2.890611442640554,
    -0.4570457994644658,
    0.3731763325901154,
    -0.4570457994644658,
    1.445305721320277,
    -0.5900435899266435,
)
DILATION = 0.3
SMOOTHING = 0.0001
SSIM_FIRST = 0.0001
SSIM_SECOND = 0.0009


def with_halo(x, sides, width):
    for axis, dim in sides:
        devices, length = (lax.axis_size(axis), x.shape[dim])
        up = [(i, (i + 1) % devices) for i in range(devices - 1)]
        down = [(j, i) for i, j in up]
        last = lax.slice_in_dim(x, length - width, length, axis=dim)
        first = lax.slice_in_dim(x, 0, width, axis=dim)
        before = lax.ppermute(last, axis, up)
        after = lax.ppermute(first, axis, down)
        x = jnp.concatenate([before, x, after], axis=dim)
    return x


def camera_rotation(angles):
    cos_a, sin_a = (jnp.cos(angles[0]), jnp.sin(angles[0]))
    cos_b, sin_b = (jnp.cos(angles[1]), jnp.sin(angles[1]))
    cos_c, sin_c = (jnp.cos(angles[2]), jnp.sin(angles[2]))
    return [
        [cos_c * cos_b, cos_c * sin_b * sin_a - sin_c * cos_a, cos_c * sin_b * cos_a + sin_c * sin_a],
        [sin_c * cos_b, sin_c * sin_b * sin_a + cos_c * cos_a, sin_c * sin_b * cos_a - cos_c * sin_a],
        [-sin_b, cos_b * sin_a, cos_b * cos_a],
    ]


def harmonics(view_axis):
    axis_x, axis_y, axis_z = (view_axis[0], view_axis[1], view_axis[2])
    sq_x, sq_y, sq_z = (axis_x * axis_x, axis_y * axis_y, axis_z * axis_z)
    return [
        SH_ZERO * jnp.ones_like(axis_x),
        -SH_ONE * axis_y,
        SH_ONE * axis_z,
        -SH_ONE * axis_x,
        SH_TWO[0] * axis_x * axis_y,
        SH_TWO[1] * axis_y * axis_z,
        SH_TWO[2] * (2.0 * sq_z - sq_x - sq_y),
        SH_TWO[3] * axis_x * axis_z,
        SH_TWO[4] * (sq_x - sq_y),
        SH_THREE[0] * axis_y * (3.0 * sq_x - sq_y),
        SH_THREE[1] * axis_x * axis_y * axis_z,
        SH_THREE[2] * axis_y * (4.0 * sq_z - sq_x - sq_y),
        SH_THREE[3] * axis_z * (2.0 * sq_z - 3.0 * sq_x - 3.0 * sq_y),
        SH_THREE[4] * axis_x * (4.0 * sq_z - sq_x - sq_y),
        SH_THREE[5] * axis_z * (sq_x - sq_y),
        SH_THREE[6] * axis_x * (sq_x - 3.0 * sq_y),
    ]


def geometry(rows, turns, centre_x, centre_y):
    scales = [jnp.exp(rows[i]) for i in range(3, 6)]
    quat = rows[6:10]
    length = jnp.sqrt(quat[0] * quat[0] + quat[1] * quat[1] + quat[2] * quat[2] + quat[3] * quat[3])
    part_w, part_x, part_y, part_z = [q / length for q in quat]
    spin = [
        [
            1.0 - 2.0 * (part_y * part_y + part_z * part_z),
            2.0 * (part_x * part_y - part_w * part_z),
            2.0 * (part_x * part_z + part_w * part_y),
        ],
        [
            2.0 * (part_x * part_y + part_w * part_z),
            1.0 - 2.0 * (part_x * part_x + part_z * part_z),
            2.0 * (part_y * part_z - part_w * part_x),
        ],
        [
            2.0 * (part_x * part_z - part_w * part_y),
            2.0 * (part_y * part_z + part_w * part_x),
            1.0 - 2.0 * (part_x * part_x + part_y * part_y),
        ],
    ]
    local = [[spin[r][c] * scales[c] for c in range(3)] for r in range(3)]
    opacity = 1.0 / (1.0 + jnp.exp(-rows[10]))
    shift_x = rows[0] - centre_x
    shift_y = rows[1] - centre_y
    records = []
    for turn in turns:
        frame = [
            [
                turn[r][0] * local[0][c] + turn[r][1] * local[1][c] + turn[r][2] * local[2][c]
                for c in range(3)
            ]
            for r in range(2)
        ]
        cov_xx = sum(frame[0][c] * frame[0][c] for c in range(3)) + DILATION
        cov_xy = sum(frame[0][c] * frame[1][c] for c in range(3))
        cov_yy = sum(frame[1][c] * frame[1][c] for c in range(3)) + DILATION
        inverse = 1.0 / (cov_xx * cov_yy - cov_xy * cov_xy)
        mean_u = turn[0][0] * shift_x + turn[0][1] * shift_y + turn[0][2] * rows[2] + centre_x
        mean_w = turn[1][0] * shift_x + turn[1][1] * shift_y + turn[1][2] * rows[2] + centre_y
        records.append(
            [mean_u, mean_w, cov_yy * inverse, -cov_xy * inverse, cov_xx * inverse, opacity]
        )
    return records


def split_parts(value):
    high = value.astype(jnp.bfloat16)
    rest = value - high.astype(jnp.float32)
    middle = rest.astype(jnp.bfloat16)
    low = (rest - middle.astype(jnp.float32)).astype(jnp.bfloat16)
    return jnp.concatenate([high, middle, low], axis=0)


def chunk_of(total):
    return 256 if total % 256 == 0 else total


def one_hot(lists_ref, start, chunk, splats):
    wanted = lists_ref[:, pl.ds(start, chunk)]
    rows = lax.broadcasted_iota(jnp.int32, (splats, chunk), 0)
    return jnp.where(rows == wanted, 1.0, 0.0).astype(jnp.bfloat16)


def project_kernel(centre_x, centre_y, params_ref, lists_ref, camera_ref, extra_ref, out_ref, rec_ref, parts_ref):
    splats = params_ref.shape[1]
    total = lists_ref.shape[1]
    turn = camera_rotation([camera_ref[:, i : i + 1] for i in range(3)])
    rows = [params_ref[i : i + 1, :] for i in range(11)]
    record = geometry(rows, [turn], centre_x, centre_y)[0]
    basis = harmonics(turn[2])
    colour = 0.5 + basis[0] * params_ref[11:14, :]
    for i in range(1, 16):
        colour = colour + basis[i] * params_ref[11 + 3 * i : 14 + 3 * i, :]
    rec_ref[...] = jnp.zeros_like(rec_ref)
    for i in range(6):
        rec_ref[i : i + 1, :] = record[i]
    rec_ref[6:9, :] = colour
    parts_ref[...] = split_parts(rec_ref[...])
    chunk = chunk_of(total)

    def step(index, carry):
        start = pl.multiple_of(index * chunk, chunk)
        picked = jnp.dot(
            parts_ref[...],
            one_hot(lists_ref, start, chunk, splats),
            preferred_element_type=jnp.float32,
        )
        out_ref[:, pl.ds(start, chunk)] = picked[0:16] + picked[16:32] + picked[32:48]
        return carry

    lax.fori_loop(0, total // chunk, step, 0)
    out_ref[9:10, :] = extra_ref[...]


def unpick_kernel(grads_ref, lists_ref, camera_ref, out_ref, acc_ref):
    splats = out_ref.shape[1]
    total = lists_ref.shape[1]
    chunk = chunk_of(total)
    acc_ref[...] = jnp.zeros_like(acc_ref)

    def step(index, carry):
        start = pl.multiple_of(index * chunk, chunk)
        acc_ref[...] += lax.dot_general(
            split_parts(grads_ref[:, pl.ds(start, chunk)]),
            one_hot(lists_ref, start, chunk, splats),
            (((1,), (1,)), ((), ())),
            preferred_element_type=jnp.float32,
        )
        return carry

    lax.fori_loop(0, total // chunk, step, 0)
    out_ref[...] = acc_ref[0:16, :] + acc_ref[16:32, :] + acc_ref[32:48, :]
    for i in range(3):
        out_ref[9 + i : 10 + i, :] = jnp.broadcast_to(camera_ref[:, i : i + 1], (1, splats))


def unproject_kernel(centre_x, centre_y, params_ref, grads_ref, out_ref):
    views = grads_ref.shape[0]
    turns = [
        camera_rotation([grads_ref[v, 9 + i : 10 + i, 0:1] for i in range(3)]) for v in range(views)
    ]
    rows = [params_ref[i : i + 1, :] for i in range(11)]
    pull = jax.vjp(lambda r: geometry(r, turns, centre_x, centre_y), rows)[1]
    cotangents = [[grads_ref[v, i : i + 1, :] for i in range(6)] for v in range(views)]
    for i, value in enumerate(pull(cotangents)[0]):
        out_ref[i : i + 1, :] = value
    bases = [harmonics(turn[2]) for turn in turns]
    colours = [grads_ref[v, 6:9, :] for v in range(views)]
    for i in range(16):
        value = bases[0][i] * colours[0]
        for v in range(1, views):
            value = value + bases[v][i] * colours[v]
        out_ref[11 + 3 * i : 14 + 3 * i, :] = value


def whole_call(kernel, name, shape, scratch, *args):
    return pl.pallas_call(
        kernel,
        name=name,
        out_shape=jax.ShapeDtypeStruct(shape, jnp.float32),
        in_specs=[pl.BlockSpec(memory_space=pltpu.VMEM)] * len(args),
        out_specs=pl.BlockSpec(memory_space=pltpu.VMEM),
        scratch_shapes=scratch,
    )(*args)


def render(gathered, grid_x, grid_y):
    delta_x = grid_x[:, None, :] - gathered[0][:, :, None]
    delta_y = grid_y[:, None, :] - gathered[1][:, :, None]
    powers = 0.5 * (
        gathered[2][:, :, None] * delta_x * delta_x
        + 2.0 * gathered[3][:, :, None] * delta_x * delta_y
        + gathered[4][:, :, None] * delta_y * delta_y
    )
    alphas = gathered[5][:, :, None] * jnp.exp(-powers)
    kept_log = jnp.log1p(-alphas)
    before = jnp.cumsum(kept_log, axis=1) - kept_log
    weights = alphas * jnp.exp(before)
    colour = jnp.einsum("skp,csk->scp", weights, gathered[6:9], precision=HIGHEST)
    return jnp.concatenate([colour, jnp.sum(kept_log, axis=1)[:, None, :]], axis=1)


def pixel_grid(owners, blocks_used, strip_rows, block_cols):
    inner = jnp.arange(128, dtype=jnp.int32)
    corner_y = owners * strip_rows + blocks_used // block_cols * 8
    corner_x = blocks_used % block_cols * 16
    grid_y = (corner_y[:, None] + inner[None, :] // 16).astype(jnp.float32) + 0.5
    grid_x = (corner_x[:, None] + inner[None, :] % 16).astype(jnp.float32) + 0.5
    return (grid_x, grid_y)


def composite(pieces, target_ids, depth_ranks, backdrop, block_rows, block_cols):
    block_count = block_rows * block_cols
    onehot = (
        target_ids[:, :, None] == jnp.arange(block_count, dtype=jnp.int32)[None, None, :]
    ).astype(jnp.float32)
    dense = jnp.einsum("scb,scqp->bsqp", onehot, pieces, precision=HIGHEST)
    kept_log = dense[:, :, 3]
    nearer = (depth_ranks[None, :] < depth_ranks[:, None]).astype(jnp.float32)
    before = jnp.einsum("st,btp->bsp", nearer, kept_log, precision=HIGHEST)
    picture = jnp.einsum("bsp,bscp->bcp", jnp.exp(before), dense[:, :, 0:3], precision=HIGHEST)
    picture = picture + backdrop[None, :, None] * jnp.exp(jnp.sum(kept_log, axis=1))[:, None, :]
    picture = picture.reshape(block_rows, block_cols, 3, 8, 16).transpose(2, 0, 3, 1, 4)
    return picture.reshape(3, block_rows * 8, block_cols * 16)


def blur_taps():
    raw_taps = [math.exp(-(offset - 5) * (offset - 5) / 4.5) for offset in range(11)]
    total = sum(raw_taps)
    return [value / total for value in raw_taps]


def blur(values, count):
    taps = blur_taps()
    width_px = values.shape[2]
    padded = jnp.pad(values, ((0, 0), (0, 0), (5, 5)))
    across = taps[0] * padded[:, :, 0:width_px]
    for offset in range(1, 11):
        across = across + taps[offset] * padded[:, :, offset : offset + width_px]
    result = taps[0] * across[:, 0:count]
    for offset in range(1, 11):
        result = result + taps[offset] * across[:, offset : offset + count]
    return result


def pixel_terms(picture, goal, count):
    mean_a = blur(picture, count)
    mean_b = blur(goal, count)
    var_a = blur(picture * picture, count) - mean_a * mean_a
    var_b = blur(goal * goal, count) - mean_b * mean_b
    cov_ab = blur(picture * goal, count) - mean_a * mean_b
    ssim = (
        (2.0 * mean_a * mean_b + SSIM_FIRST)
        * (2.0 * cov_ab + SSIM_SECOND)
        / ((mean_a * mean_a + mean_b * mean_b + SSIM_FIRST) * (var_a + var_b + SSIM_SECOND))
    )
    differ = picture[:, 5 : 5 + count] - goal[:, 5 : 5 + count]
    return 0.8 * jnp.sqrt(differ * differ + SMOOTHING) + 0.2 * (1.0 - ssim)


def shards(params, visible, blocks, counts, depth_rank, camera, background, target):
    devices = lax.axis_size("space")
    me_index = lax.axis_index("space")
    slot_total = visible.shape[1]
    list_length = visible.shape[2]
    capacity = slot_total // devices
    strip_rows = target.shape[2]
    width_px = target.shape[3]
    block_rows = strip_rows // 8
    block_cols = width_px // 16
    height_px = strip_rows * devices
    splats = params.shape[1]
    lists = visible[0].reshape(1, slot_total * list_length)
    live = jnp.arange(capacity, dtype=jnp.int32)[None, :] < counts[0][:, None]
    target_ids = jnp.where(live, blocks[0].reshape(devices, capacity), -1).astype(jnp.float32)
    id_row = jnp.broadcast_to(target_ids[:, :, None], (devices, capacity, list_length))
    centre_x = 0.5 * width_px
    centre_y = 0.5 * height_px
    message = whole_call(
        functools.partial(project_kernel, centre_x, centre_y),
        "project",
        (16, slot_total * list_length),
        [pltpu.VMEM((16, splats), jnp.float32), pltpu.VMEM((48, splats), jnp.bfloat16)],
        params,
        lists,
        camera,
        id_row.reshape(1, slot_total * list_length),
    )
    message = message[0:10].reshape(10, devices, capacity * list_length).transpose(1, 0, 2)
    received = lax.all_to_all(message, "space", split_axis=0, concat_axis=0, tiled=True)
    recv_ids = received[:, 9].reshape(devices, capacity, list_length)[:, :, 0].astype(jnp.int32)
    own_blocks = jnp.maximum(recv_ids.reshape(devices * capacity), 0)
    grid_x, grid_y = pixel_grid(
        jnp.full(own_blocks.shape, me_index, jnp.int32), own_blocks, strip_rows, block_cols
    )

    def owner_side(recv_in):
        gathered = (
            recv_in.reshape(devices, 9, capacity, list_length)
            .transpose(1, 0, 2, 3)
            .reshape(9, devices * capacity, list_length)
        )
        pieces = render(gathered, grid_x, grid_y).reshape(devices, capacity, 4, 128)
        return composite(pieces, recv_ids, depth_rank[0], background[0], block_rows, block_cols)

    strip, pull_owner = jax.vjp(owner_side, received[:, 0:9])
    stacked = jnp.concatenate([strip, target[0]], axis=0)
    extended = with_halo(stacked, (("space", 1),), 10)
    goal = extended[3:6]
    rows_here = strip_rows + 10
    terms, pull_terms = jax.vjp(lambda p: pixel_terms(p, goal, rows_here), extended[0:3])
    own_loss = jnp.sum(terms[:, 5 : 5 + strip_rows])
    row_ids = jnp.arange(rows_here, dtype=jnp.int32) + me_index * strip_rows - 5
    inside = ((row_ids >= 0) & (row_ids < height_px)).astype(jnp.float32)
    ones = jnp.broadcast_to(inside[None, :, None], terms.shape)
    grad_strip = pull_terms(ones)[0][:, 10 : 10 + strip_rows]
    grad_received = pull_owner(grad_strip)[0]
    loss_row = jnp.broadcast_to(own_loss, (devices, 1, capacity * list_length))
    returned = lax.all_to_all(
        jnp.concatenate([grad_received, loss_row], axis=1),
        "space",
        split_axis=0,
        concat_axis=0,
        tiled=True,
    )
    loss_sum = jnp.sum(returned[:, 9, 0])
    grad_slots = returned.transpose(1, 0, 2).reshape(10, slot_total * list_length)
    grad_slots = jnp.pad(grad_slots[0:9], ((0, 7), (0, 0)))
    grad_records = whole_call(
        unpick_kernel,
        "unpick",
        (16, splats),
        [pltpu.VMEM((48, splats), jnp.float32)],
        grad_slots,
        lists,
        camera,
    )
    every_view = lax.all_gather(grad_records, "view", axis=0, tiled=False)
    grad_params = whole_call(
        functools.partial(unproject_kernel, centre_x, centre_y),
        "unproject",
        params.shape,
        [],
        params,
        every_view,
    )
    loss_value = (loss_sum / (3.0 * height_px * width_px)).reshape(1)
    return (grad_params, strip[None], loss_value)


def solution(mesh):
    in_specs = (
        P(None, "space"),
        P("space", None, None),
        P("space", None),
        P("space", None),
        P("view", None),
        P("view", None),
        P("view", None),
        P("view", None, "space", None),
    )
    out_specs = (P(None, "space"), P("view", None, "space", None), P("view"))
    return jax.shard_map(shards, mesh=mesh, in_specs=in_specs, out_specs=out_specs, check_vma=False)
```
